32 devices in a mesh: row: 4 (over y, x), col: 8 (over z, core).
Axes of the slice: x: 2, y: 2, z: 4, core: 2. Of those that a mesh axis runs over, the one named last changes fastest.
Arguments:
- root_inverse: float32 [12288, 12288], P('row', 'col'), may hold values from -6 to 6, as said below
- panel_root: float32 [2, 12288, 256], P(None, ('row', 'col')), may hold values from -0.0546875 to 0.0546875
- panel_tail: float32 [1, 256, 256], replicated, may hold values from -0.375 to 0.375
- factor_inverse: float32 [2, 256, 256], replicated, may hold values from -1 to 2, as said below
- ancestors: int32 [84], replicated, may hold values from 0 to 95, as said below
Outputs:
- border: float32 [2, 12288, 256], P(None, ('row', 'col'))
- border_tail: float32 [1, 256, 256], replicated
- diagonal: float32 [2, 256, 256], replicated
The draws below stay inside these ranges and needn't reach their ends.
Inputs may be any that keep to these rules, and one draw needn't show every extreme that they name: `ancestors`: each of the two lists is increasing and holds distinct root blocks; the list of supernode 1 is a subset of that of supernode 0. `factor_inverse`: each block is lower triangular with a positive diagonal. `root_inverse`: the matrix is symmetric.
All inputs are finite; a program needn't handle non-finite values.
Results may differ from the reference program's by a relative error of at most 0.0001.
Values sent between devices are 32-bit elements; how exact they have to be, the bound alone decides.
No kernel may reach another device: no remote copies, remote signals or barrier semaphores. Data moves between devices by JAX's collectives and lax.ppermute only.
A program may use at most 64 MiB of HBM per device.

```python
import math
import jax
import jax.numpy as jnp
from jax import lax

R = 12288
W = 256
BLK = 128


def draw_ancestors(key, part):
    nblocks = R // BLK
    first_count = nblocks // 2
    second_count = 3 * nblocks // 8
    order = jax.random.permutation(jax.random.fold_in(key, 11), nblocks)
    first = jnp.sort(order[:first_count])
    pick = jax.random.permutation(jax.random.fold_in(key, 12), first_count)
    second = jnp.sort(first[pick[:second_count]])
    return jnp.concatenate([first, second]).astype(jnp.int32)


def draw_factor_inverse(key, part):
    key_diag = jax.random.fold_in(key, 21)
    key_low = jax.random.fold_in(key, 22)
    diag_values = jax.random.uniform(key_diag, (2, W), jnp.float32, 0.5, 1.5)
    lower = jax.random.uniform(key_low, (2, W, W), jnp.float32, -1.0, 1.0) * (0.9 / math.sqrt(W))
    eye = jnp.eye(W, dtype=jnp.float32)
    return (jnp.tril(lower, -1) + diag_values[:, :, None] * eye[None, :, :]).astype(jnp.float32)


def draw_root_inverse(key, part):
    key_main = jax.random.fold_in(key, 31)
    base = jax.random.normal(key_main, (R, R), jnp.float32)
    whole = (base + base.T) * (1.0 / math.sqrt(2.0))
    return jnp.clip(whole, -6.0, 6.0).astype(jnp.float32)


def steps_of(rng, dims, cuts, smallest, top_value):
    gain, own = 1.0, jax.random.fold_in(rng, 6)
    for axis_at, shards_of in cuts:
        heights = jnp.exp(jax.random.uniform(jax.random.fold_in(own, axis_at), (shards_of,), jnp.float32, smallest / len(cuts), top_value / len(cuts)))
        gain = gain * jnp.repeat(heights, dims[axis_at] // shards_of).reshape([-1 if axis == axis_at else 1 for axis in range(len(dims))])
    return gain


def normal_values(stream_key, extent, deviation, reach, split=(), held_as=jnp.bfloat16):
    level = steps_of(stream_key, extent, split, -0.22, 0.18) if split else 1.0
    result = jax.random.normal(stream_key, extent, jnp.float32) * deviation * level
    return jnp.minimum(jnp.maximum(result, -reach), reach).astype(held_as)


def setup_inputs(seed: int = 0) -> dict:
    key_of = jax.random.split(jax.random.key(seed), 6)
    return {
        "root_inverse": draw_root_inverse(jax.random.fold_in(key_of[5], 71), 0),
        "panel_root": normal_values(key_of[1], (2, R, W), R ** -0.5, 0.0546875, ((1, 32),), jnp.float32),
        "panel_tail": normal_values(key_of[2], (1, W, W), W ** -0.5, 0.375, (), jnp.float32),
        "factor_inverse": draw_factor_inverse(jax.random.fold_in(key_of[5], 71), 0),
        "ancestors": draw_ancestors(jax.random.fold_in(key_of[5], 71), 0),
    }


def product(left, right):
    return jnp.dot(left, right, precision=lax.Precision.HIGHEST, preferred_element_type=jnp.float32)


def tail_slot(later, earlier):
    return later * (later - 1) // 2 + earlier


def reference(root_inverse, panel_root, panel_tail, factor_inverse, ancestors):
    nblocks = R // BLK
    counts = [nblocks // 2, 3 * nblocks // 8]
    blocks = jnp.arange(R, dtype=jnp.int32) // BLK
    borders = []
    diagonals = []
    tails = [None]

    def inner(first, second):
        if first == second:
            return diagonals[first]
        if first < second:
            return tails[tail_slot(second, first)]
        return tails[tail_slot(first, second)].T

    start = 0
    for node in range(2):
        listed = ancestors[start:start + counts[node]]
        start = start + counts[node]
        mask = jnp.any(blocks[:, None] == listed[None, :], axis=1).astype(jnp.float32)[:, None]
        panel = panel_root[node] * mask
        image = product(root_inverse, panel)
        for prior in range(node):
            image = image + product(borders[prior], panel_tail[tail_slot(node, prior)])
        cross = []
        for prior in range(node):
            value = product(borders[prior].T, panel)
            for other in range(node):
                value = value + product(inner(prior, other), panel_tail[tail_slot(node, other)])
            cross.append(value)
        block = product(factor_inverse[node].T, factor_inverse[node]) + product(panel.T, image)
        for prior in range(node):
            block = block + product(panel_tail[tail_slot(node, prior)].T, cross[prior])
        for prior in range(node):
            tails[tail_slot(node, prior)] = -cross[prior]
        borders.append(-(mask * image))
        diagonals.append(block)
    return jnp.stack(borders), jnp.stack(tails), jnp.stack(diagonals)
```

```python
import jax
import jax.numpy as jnp
from jax import lax
from jax.sharding import PartitionSpec as P

BLK = 128


def product(left, right, precision=lax.Precision.HIGHEST):
    return jnp.dot(left, right, precision=precision, preferred_element_type=jnp.float32)


def over_rows(left, right, precision=lax.Precision.HIGHEST):
    return lax.dot_general(
        left, right, (((0,), (0,)), ((), ())), precision=precision, preferred_element_type=jnp.float32
    )


def member(start, count, listed):
    block_ids = (start + lax.iota(jnp.int32, count)) // BLK
    return jnp.any(block_ids[:, None] == listed[None, :], axis=1).astype(jnp.float32)[:, None]


def tree_sum(parts):
    while len(parts) > 1:
        parts = [parts[k] + parts[k + 1] for k in range(0, len(parts), 2)]
    return parts[0]


def pick(index, parts):
    value = parts[0]
    for k in range(1, len(parts)):
        value = jnp.where(index == k, parts[k], value)
    return value


class Slice:
    def __init__(self, mesh):
        self.rows = mesh.shape["row"]
        self.cols = mesh.shape["col"]
        self.planes = self.cols // 2

    def across(self, x, step):
        return lax.ppermute(x, "row", [(r, r ^ step) for r in range(self.rows)])

    def swap(self, x):
        return lax.ppermute(x, "col", [(c, c ^ 1) for c in range(self.cols)])

    def along(self, x, step):
        return lax.ppermute(x, "col", [(c, c ^ (2 * step)) for c in range(self.cols)])

    def up(self, x, step):
        pairs = [(2 * z + c, 2 * z + 2 + c) for z in range(step - 1, self.planes - 1) for c in (0, 1)]
        return lax.ppermute(x, "col", pairs)

    def down(self, x, step):
        pairs = [(2 * z + c, 2 * z - 2 + c) for z in range(1, self.planes - step + 1) for c in (0, 1)]
        return lax.ppermute(x, "col", pairs)

    def home(self, x):
        pairs = []
        for r in range(self.rows):
            for c in range(self.cols):
                pairs.append((r * self.cols + c, self.rows * c + r))
        return lax.ppermute(x, ("row", "col"), pairs)


def gather_block(net, x, plane, core):
    rising, falling = [x], [x]
    for step in range(1, net.planes):
        rising.append(net.up(rising[-1], step))
        falling.append(net.down(falling[-1], step))
    mine = [x] + [rising[d] + falling[net.planes - d] for d in range(1, net.planes)]
    other = [net.swap(piece) for piece in mine]
    first = [jnp.where(core == 0, a, b) for a, b in zip(mine, other)]
    second = [jnp.where(core == 0, b, a) for a, b in zip(mine, other)]
    pairs = [jnp.concatenate([a, b], axis=0) for a, b in zip(first, second)]
    size = pairs[0].shape[0]
    backward = jnp.concatenate([pairs[(net.planes - k) % net.planes] for k in range(net.planes)] * 2, axis=0)
    start = lax.rem(net.planes - plane, net.planes) * size
    return lax.dynamic_slice_in_dim(backward, start, net.planes * size, 0)


def reduce_rows(net, x, row):
    size = x.shape[0] // net.rows
    parts = [lax.dynamic_slice_in_dim(x, row * size, size, 0)]
    for step in range(1, net.rows):
        parts.append(net.across(lax.dynamic_slice_in_dim(x, (row ^ step) * size, size, 0), step))
    return tree_sum(parts)


def reduce_all(net, x, row, core):
    half = x.shape[0] // 2
    low, high = x[:half], x[half:]
    mine = jnp.where(core == 0, low, high) + net.swap(jnp.where(core == 0, high, low))
    part = reduce_rows(net, mine, row)
    part = tree_sum([part] + [net.along(part, step) for step in range(1, net.planes)])
    got = [part] + [net.across(part, step) for step in range(1, net.rows)]
    mine = jnp.concatenate(
        [pick(row, [got[r ^ at] for r in range(net.rows)]) for at in range(net.rows)], axis=0
    )
    other = net.swap(mine)
    return jnp.concatenate(
        [jnp.where(core == 0, mine, other), jnp.where(core == 0, other, mine)], axis=0
    )


def solution(mesh):
    net = Slice(mesh)
    placed = (P("row", "col"), P(None, ("row", "col"), None), P(), P(), P())

    def local(root_inverse, panel_root, panel_tail, factor_inverse, ancestors):
        row = lax.axis_index("row")
        col = lax.axis_index("col")
        plane, core = col // 2, col % 2
        share, width = panel_root.shape[1:]
        block_rows = root_inverse.shape[0]
        nblocks = block_rows * net.rows // BLK
        count = nblocks // 2
        start = row * block_rows + col * share
        masks = [
            member(start, share, ancestors[:count]),
            member(start, share, ancestors[count:]),
        ]
        panels = [panel_root[k] * masks[k] for k in range(2)]
        tail = panel_tail[0]
        images = []
        for k in range(2):
            whole = gather_block(net, panels[k], plane, core)
            partial = over_rows(root_inverse, whole, lax.Precision.HIGH)
            images.append(net.home(reduce_rows(net, partial, row)))
        first = -(masks[0] * images[0])
        second = images[1] + product(first, tail)
        own0 = over_rows(panels[0], images[0])
        cross = over_rows(first, panels[1])
        own1 = over_rows(panels[1], second) + over_rows(tail, cross)
        total = reduce_all(net, jnp.concatenate([own0, cross, own1], axis=0), row, core)
        block0 = over_rows(factor_inverse[0], factor_inverse[0]) + total[:width]
        carried = product(block0, tail)
        crossed = total[width : 2 * width] + carried
        block1 = (
            over_rows(factor_inverse[1], factor_inverse[1])
            + total[2 * width :]
            + over_rows(tail, carried)
        )
        border = jnp.stack([first, -(masks[1] * second)])
        return border, -crossed[None], jnp.stack([block0, block1])

    return jax.shard_map(
        local,
        mesh=mesh,
        in_specs=placed,
        out_specs=(P(None, ("row", "col"), None), P(), P()),
        check_vma=False,
    )
```
